32 devices in a mesh: ctx: 8 (over z, core), head: 4 (over y, x).
Axes of the slice: x: 2, y: 2, z: 4, core: 2. Of those that a mesh axis runs over, the one named last changes fastest.
Arguments:
- q_latent: bfloat16 [1024, 1536], P('ctx', 'head'), may hold values from -72 to 72
- latent_cache: bfloat16 [1024, 576], P('ctx'), may hold values from -6 to 6
- w_q_up: bfloat16 [1536, 3072], P(None, 'head'), may hold values from -0.15625 to 0.15625
- w_kv_up: bfloat16 [512, 4096], P(None, 'head'), may hold values from -0.25 to 0.25
- w_out: bfloat16 [2048, 7168], P('head', 'ctx'), may hold values from -1 to 1
- token_pos: int32 [1024], P('ctx'), may hold values from 0 to 1023, as said below
- start_offset: int32 [1], replicated, may hold values from 0 to 65535
Outputs:
- layer_out: bfloat16 [1024, 7168], P('ctx', 'head')
The draws below stay inside these ranges and needn't reach their ends.
Inputs may be any that keep to these rules, and one draw needn't show every extreme that they name: `token_pos`: a permutation of 0 to 1023; the 128 tokens of each index of ctx hold consecutive positions in increasing order.
All inputs are finite; a program needn't handle non-finite values.
Results may differ from the reference program's by a relative error of at most 0.035.
Values may be sent and summed in bfloat16 or wider, within the bound.
A program may use at most 64 MiB of HBM per device.

```python
import jax
import jax.numpy as jnp
from jax import lax

D = 7168
QL = 1536
KVL = 512
NOPE = 128
ROPE = 64
VDIM = 128
HEAD_DEV = 4
TOK_DEV = 128
HEADS = 16
TOKENS = 1024
N_HEAD = 4


def draw_q_latent(key, part):
    first = jax.random.fold_in(key, 0)
    values = jax.random.truncated_normal(first, -6.0, 6.0, (TOKENS, QL), jnp.float32)
    return values.astype(jnp.bfloat16)


def draw_token_pos(key, part):
    blocks = TOKENS // TOK_DEV
    order = jax.random.permutation(key, blocks).astype(jnp.int32)
    inside = jnp.arange(TOK_DEV, dtype=jnp.int32)
    return (order[:, None] * TOK_DEV + inside[None, :]).reshape(TOKENS)


def steps_of(stream_key, shape, pieces, least, top_value):
    factor_of = 1.0
    for position, blocks in pieces:
        steps = jax.random.uniform(jax.random.fold_in(jax.random.fold_in(stream_key, 6), position), (blocks,), jnp.float32, least / len(pieces), top_value / len(pieces))
        factor_of = factor_of * jnp.repeat(jnp.exp(steps), shape[position] // blocks).reshape((-1,) + (1,) * (len(shape) - 1 - position))
    return factor_of


def bell_draw(rng, dims, deviation, bound, cuts=(), kind=jnp.bfloat16):
    array = jax.random.normal(rng, dims, jnp.float32) * deviation
    if len(cuts) > 0:
        array = steps_of(rng, dims, cuts, -0.22, 0.18) * array
    return jnp.clip(array, min=-bound, max=bound).astype(kind)


def setup_inputs(seed: int = 0) -> dict:
    key_of = jax.random.split(jax.random.key(seed), 8)
    q_latent = draw_q_latent(jax.random.fold_in(key_of[7], 71), 0)
    latent_cache = bell_draw(key_of[1], (TOKENS, KVL + ROPE), 1.0, 6.0, ((0, 8),))
    w_q_up = bell_draw(key_of[2], (QL, HEADS * (NOPE + ROPE)), QL ** -0.5, 0.15625, ((1, 4),))
    w_kv_up = bell_draw(key_of[3], (KVL, HEADS * (NOPE + VDIM)), KVL ** -0.5, 0.25, ((1, 4),))
    w_out = bell_draw(key_of[4], (HEADS * VDIM, D), (HEADS * VDIM // 64) ** -0.5, 1.0, ((0, 4), (1, 8)))
    token_pos = draw_token_pos(jax.random.fold_in(key_of[7], 71), 0)
    start_offset = jax.random.randint(key_of[6], (1,), 0, 65536).astype(jnp.int32)
    return {"q_latent": q_latent, "latent_cache": latent_cache, "w_q_up": w_q_up, "w_kv_up": w_kv_up, "w_out": w_out, "token_pos": token_pos, "start_offset": start_offset}


negative_fill = -1e30
softmax_scale = 0.135
rope_base = 10000.0


def rotate(values, angle):
    half = ROPE // 2
    cosine = jnp.cos(angle)
    sine = jnp.sin(angle)
    first = values[..., :half]
    second = values[..., half:]
    return jnp.concatenate([first * cosine - second * sine, first * sine + second * cosine], axis=-1)


def reference(q_latent, latent_cache, w_q_up, w_kv_up, w_out, token_pos, start_offset):
    head_count = HEAD_DEV * N_HEAD
    query = jnp.dot(q_latent, w_q_up, preferred_element_type=jnp.float32).reshape(TOKENS, head_count, NOPE + ROPE)
    absolute = (token_pos + start_offset[0]).astype(jnp.float32)
    freqs = rope_base ** (-jnp.arange(ROPE // 2, dtype=jnp.float32) * 2.0 / ROPE)
    angle = absolute[:, None, None] * freqs[None, None, :]
    query_nope = query[..., :NOPE].astype(jnp.bfloat16)
    query_rope = rotate(query[..., NOPE:], angle).astype(jnp.bfloat16)
    latent = latent_cache[:, :KVL]
    key_rope = latent_cache[:, KVL:]
    visible = token_pos[None, :] <= token_pos[:, None]

    def one_head(index):
        columns = lax.dynamic_slice_in_dim(w_kv_up, (index * (NOPE + VDIM)).astype(jnp.int32), NOPE + VDIM, 1)
        expanded = jnp.dot(latent, columns, preferred_element_type=jnp.float32).astype(jnp.bfloat16)
        head_nope = lax.dynamic_index_in_dim(query_nope, index, 1, keepdims=False)
        head_rope = lax.dynamic_index_in_dim(query_rope, index, 1, keepdims=False)
        scores = jnp.dot(head_nope, expanded[:, :NOPE].T, preferred_element_type=jnp.float32)
        scores = scores + jnp.dot(head_rope, key_rope.T, preferred_element_type=jnp.float32)
        scores = jnp.where(visible, scores * softmax_scale, negative_fill)
        largest = jnp.max(scores, axis=-1, keepdims=True)
        weights = jnp.where(visible, jnp.exp(scores - largest), 0.0)
        totals = jnp.sum(weights, axis=-1, keepdims=True)
        summed = jnp.dot(weights.astype(jnp.bfloat16), expanded[:, NOPE:], preferred_element_type=jnp.float32)
        return (summed / totals).astype(jnp.bfloat16)

    per_head = lax.map(one_head, jnp.arange(head_count, dtype=jnp.int32))
    attention = jnp.transpose(per_head, (1, 0, 2)).reshape(TOKENS, head_count * VDIM)
    group_width = HEAD_DEV * VDIM

    def one_group(index):
        start = (index * group_width).astype(jnp.int32)
        columns = lax.dynamic_slice_in_dim(attention, start, group_width, 1)
        rows = lax.dynamic_slice_in_dim(w_out, start, group_width, 0)
        return jnp.dot(columns, rows, preferred_element_type=jnp.float32).astype(jnp.bfloat16)

    def add_group(total, index):
        return total + one_group(index).astype(jnp.float32), None

    total, unused = lax.scan(add_group, jnp.zeros((TOKENS, D), jnp.float32), jnp.arange(N_HEAD, dtype=jnp.int32))
    return total.astype(jnp.bfloat16)
```

```python
import functools

import jax
import jax.numpy as jnp
from jax import lax
from jax.experimental import pallas as pl
from jax.experimental.pallas import tpu as pltpu
from jax.sharding import PartitionSpec as P

KVL = 512
NOPE = 128
ROPE = 64
VDIM = 128
LANES = 640

negative_fill = -1e30
softmax_scale = 0.135
rope_base = 10000.0
F32 = jnp.float32
BF16 = jnp.bfloat16
MESH = pl.DeviceIdType.MESH


def dot_t(a, b):
    return lax.dot_general(a, b, (((1,), (1,)), ((), ())), preferred_element_type=F32)


def kernel(
    n_c, n_h, heads, rows,
    qlat, lat, wq, wkv, wout, cos, sin, qpos,
    out,
    wq_v, wkv_v, w2, qbuf, latbuf, qa, score, prob, attbuf, pbuf, rsbuf, rbuf, zbuf,
    lsem, qs, qr, lzs, lps, latr, ws, wr, ats, atr, rss, rsr, zs, zr, os_, or_,
):
    n_z = n_c // 2
    piece = rows // n_h
    width = w2.shape[2]
    q_block = qbuf.shape[2]
    c = lax.axis_index("ctx")
    h = lax.axis_index("head")
    k = lax.rem(c, 2)
    z = lax.div(c, 2)
    partner = c + 1 - 2 * k
    z_of = [lax.rem(z + d, n_z) for d in range(n_z)]
    h_of = [lax.rem(h + e, n_h) for e in range(n_h)]
    c_of = [2 * zz + k for zz in z_of]

    def remote(src, dst, ssem, rsem, cc, hh):
        return pltpu.make_async_remote_copy(
            src_ref=src, dst_ref=dst, send_sem=ssem, recv_sem=rsem,
            device_id=(cc, hh), device_id_type=MESH,
        )

    def slot(cc):
        return latbuf.at[pl.ds(pl.multiple_of(cc * rows, rows), rows), :]

    barrier = pltpu.get_barrier_semaphore()
    for d in range(1, n_z):
        pl.semaphore_signal(barrier, inc=1, device_id=(c_of[d], h), device_id_type=MESH)
    for e in range(1, n_h):
        pl.semaphore_signal(barrier, inc=1, device_id=(c, h_of[e]), device_id_type=MESH)
    pl.semaphore_signal(barrier, inc=1, device_id=(partner, h), device_id_type=MESH)

    local = [
        pltpu.make_async_copy(qlat, qbuf.at[h], lsem.at[0]),
        pltpu.make_async_copy(wq, wq_v, lsem.at[1]),
        pltpu.make_async_copy(wkv, wkv_v, lsem.at[2]),
        pltpu.make_async_copy(lat, slot(c), lsem.at[3]),
        pltpu.make_async_copy(wout, w2.at[k], lsem.at[4]),
    ]
    for copy in local:
        copy.start()
    pl.semaphore_wait(barrier, n_z + n_h - 1)

    sends = []

    def send(*args):
        copy = remote(*args)
        copy.start()
        sends.append(copy)

    for e in range(1, n_h):
        send(qlat, qbuf.at[h], qs.at[e], qr.at[h], c, h_of[e])
    for d in range(n_z - 1, 0, -1):
        send(lat, slot(c), lzs.at[d], latr.at[c], c_of[d], h)
    send(lat, slot(c), lps.at[0], latr.at[c], partner, h)

    local[0].wait()
    local[1].wait()
    for e in range(1, n_h):
        remote(qlat, qbuf.at[h_of[e]], qs.at[e], qr.at[h_of[e]], c, h_of[e]).wait_recv()
    query = None
    for g in range(n_h):
        term = jnp.dot(qbuf[g], wq_v[g * q_block:(g + 1) * q_block, :], preferred_element_type=F32)
        query = term if query is None else query + term
    local[2].wait()
    for j in range(heads):
        base = j * (NOPE + ROPE)
        nope = query[:, base:base + NOPE].astype(BF16)
        main = dot_t(nope, wkv_v[:, j * 256:j * 256 + NOPE])
        lines = slice(j * rows, (j + 1) * rows)
        qa[lines, 0:KVL] = main.astype(BF16)
        rope = query[:, base + NOPE:base + NOPE + ROPE]
        half = ROPE // 2
        swapped = jnp.concatenate([rope[:, half:], rope[:, :half]], axis=1)
        rotated = rope * cos[...] + swapped * sin[...]
        qa[lines, KVL:LANES] = jnp.concatenate(
            [rotated.astype(BF16), jnp.zeros((rows, LANES - KVL - ROPE), BF16)], axis=1
        )

    for d in range(1, n_z):
        remote(lat, slot(c_of[d]), lzs.at[d], latr.at[c_of[d]], c_of[d], h).wait_recv()
        send(slot(c_of[d]), slot(c_of[d]), lps.at[d], latr.at[c_of[d]], partner, h)
    send(wout, w2.at[k], ws, wr, partner, h)
    local[3].wait()
    for d in range(n_z):
        cc = 2 * z_of[d] + 1 - k
        remote(lat, slot(cc), lps.at[d], latr.at[cc], partner, h).wait_recv()

    lane = lax.broadcasted_iota(jnp.int32, (8, 128), 1)
    pick = jnp.where(lane == ROPE, 64.0, jnp.where(lane == ROPE + 1, 1.0, 0.0)).astype(BF16)
    kpos = dot_t(pick, latbuf[:, KVL:LANES])[0:1, :]
    score[...] = dot_t(qa[...], latbuf[...])
    visible = kpos <= qpos[:, 0:1]
    sums = []
    for j in range(heads):
        lines = slice(j * rows, (j + 1) * rows)
        s = jnp.where(visible, score[lines, :] * softmax_scale, negative_fill)
        largest = jnp.max(s, axis=-1, keepdims=True)
        weights = jnp.where(visible, jnp.exp(s - largest), 0.0)
        sums.append(jnp.sum(weights, axis=-1, keepdims=True))
        prob[lines, :] = weights.astype(BF16)
    summed = jnp.dot(prob[...], latbuf[:, 0:KVL], preferred_element_type=F32)
    for j in range(heads):
        normed = (summed[j * rows:(j + 1) * rows, :] / sums[j]).astype(BF16)
        value = jnp.dot(normed, wkv_v[:, j * 256 + NOPE:(j + 1) * 256], preferred_element_type=F32)
        attbuf[z, :, j * VDIM:(j + 1) * VDIM] = value.astype(BF16)

    for d in range(n_z - 1, 0, -1):
        send(attbuf.at[z], attbuf.at[z], ats.at[d], atr.at[z], c_of[d], h)

    local[4].wait()
    remote(wout, w2.at[1 - k], ws, wr, partner, h).wait_recv()
    for d in range(n_z):
        zz = z_of[d]
        if d > 0:
            remote(attbuf.at[zz], attbuf.at[zz], ats.at[d], atr.at[zz], c_of[d], h).wait_recv()
        for m in range(2):
            part = jnp.dot(attbuf[zz], w2[m], preferred_element_type=F32).astype(BF16)
            for i in range(n_h):
                pbuf[zz, i, :, m * width:(m + 1) * width] = part[i * piece:(i + 1) * piece, :]
        for e in range(1, n_h):
            send(pbuf.at[zz, h_of[e]], rsbuf.at[zz, h], rss.at[d, e], rsr.at[zz, h], c, h_of[e])

    for d in range(n_z):
        zz = z_of[d]
        total = pbuf[zz, h].astype(F32)
        for e in range(1, n_h):
            hh = h_of[e]
            remote(pbuf.at[zz, hh], rsbuf.at[zz, hh], rss.at[d, e], rsr.at[zz, hh], c, hh).wait_recv()
            total = total + rsbuf[zz, hh].astype(F32)
        if d == 0:
            zbuf[z] = total.astype(BF16)
        else:
            rbuf[d] = total.astype(BF16)
            send(rbuf.at[d], zbuf.at[z], zs.at[d], zr.at[z], c_of[d], h)

    for e in range(1, n_h + 1):
        zz = h_of[e % n_h]

        @pl.when(zz != z)
        def _():
            remote(rbuf.at[0], zbuf.at[zz], zs.at[0], zr.at[zz], partner, h).wait_recv()

        if e < n_h:
            send(zbuf.at[zz], out.at[h], os_.at[e], or_.at[h], c, zz)
        else:
            out[h] = zbuf[h]
    for e in range(1, n_h):
        hh = h_of[e]
        remote(zbuf.at[0], out.at[hh], os_.at[e], or_.at[hh], c, hh).wait_recv()
    for copy in sends:
        copy.wait_send()


def shards(n_c, n_h, q_latent, latent_cache, w_q_up, w_kv_up, w_out, token_pos, start_offset):
    rows, q_block = q_latent.shape
    heads = w_q_up.shape[1] // (NOPE + ROPE)
    n_z = n_c // 2
    assert n_z == n_h
    keys = n_c * rows
    width = w_out.shape[1]
    piece = rows // n_h
    absolute = (token_pos + start_offset[0]).astype(F32)
    freqs = rope_base ** (-jnp.arange(ROPE // 2, dtype=F32) * 2.0 / ROPE)
    angle = absolute[:, None] * freqs[None, :]
    cosine, sine = jnp.cos(angle), jnp.sin(angle)
    cos = jnp.concatenate([cosine, cosine], axis=1)
    sin = jnp.concatenate([-sine, sine], axis=1)
    qpos = jnp.broadcast_to(token_pos.astype(F32)[:, None], (rows, 128))
    lat = jnp.concatenate(
        [
            latent_cache,
            (token_pos // 64).astype(BF16)[:, None],
            (token_pos % 64).astype(BF16)[:, None],
            jnp.zeros((rows, LANES - KVL - ROPE - 2), BF16),
        ],
        axis=1,
    )
    dma = pltpu.SemaphoreType.DMA
    anywhere = pl.BlockSpec(memory_space=pl.ANY)
    vmem = pl.BlockSpec(memory_space=pltpu.VMEM)
    result = pl.pallas_call(
        functools.partial(kernel, n_c, n_h, heads, rows),
        out_shape=jax.ShapeDtypeStruct((n_h, piece, 2 * width), BF16),
        in_specs=[anywhere] * 5 + [vmem] * 3,
        out_specs=vmem,
        scratch_shapes=[
            pltpu.VMEM(w_q_up.shape, BF16),
            pltpu.VMEM(w_kv_up.shape, BF16),
            pltpu.VMEM((2,) + w_out.shape, BF16),
            pltpu.VMEM((n_h, rows, q_block), BF16),
            pltpu.VMEM((keys, LANES), BF16),
            pltpu.VMEM((heads * rows, LANES), BF16),
            pltpu.VMEM((heads * rows, keys), F32),
            pltpu.VMEM((heads * rows, keys), BF16),
            pltpu.VMEM((n_z, rows, heads * VDIM), BF16),
            pltpu.VMEM((n_z, n_h, piece, 2 * width), BF16),
            pltpu.VMEM((n_z, n_h, piece, 2 * width), BF16),
            pltpu.VMEM((n_z, piece, 2 * width), BF16),
            pltpu.VMEM((n_z, piece, 2 * width), BF16),
            dma((5,)),
            dma((n_h,)), dma((n_h,)),
            dma((n_z,)), dma((n_z,)), dma((n_c,)),
            dma, dma,
            dma((n_z,)), dma((n_z,)),
            dma((n_z, n_h)), dma((n_z, n_h)),
            dma((n_z,)), dma((n_z,)),
            dma((n_h,)), dma((n_h,)),
        ],
        compiler_params=pltpu.CompilerParams(
            collective_id=0, has_side_effects=True, vmem_limit_bytes=60 * 1024 * 1024
        ),
        name="mla",
    )(q_latent, lat, w_q_up, w_kv_up, w_out, cos, sin, qpos)
    return result.reshape(rows, 2 * width)


def solution(mesh):
    in_specs = (
        P("ctx", "head"),
        P("ctx", None),
        P(None, "head"),
        P(None, "head"),
        P("head", "ctx"),
        P("ctx"),
        P(),
    )
    out_specs = P("ctx", "head")
    body = functools.partial(shards, mesh.shape["ctx"], mesh.shape["head"])
    return jax.shard_map(body, mesh=mesh, in_specs=in_specs, out_specs=out_specs, check_vma=False)
```

```python
import functools

import jax
import jax.numpy as jnp
from jax import lax
from jax.experimental import pallas as pl
from jax.experimental.pallas import tpu as pltpu
from jax.sharding import PartitionSpec as P

KVL = 512
NOPE = 128
ROPE = 64
VDIM = 128
LANES = KVL + ROPE

negative_fill = -1e30
softmax_scale = 0.135
rope_base = 10000.0
F32 = jnp.float32
BF16 = jnp.bfloat16
MESH = pl.DeviceIdType.MESH


def dot_t(a, b):
    return lax.dot_general(a, b, (((1,), (1,)), ((), ())), preferred_element_type=F32)


def kernel(
    n_c, n_h, heads, rows,
    qlat, lat, wq, wkv, wout, cos, sin, kpos, qpos,
    out,
    wq_v, wkv_v, w2, qbuf, latbuf, posbuf, qa, score, prob, attbuf,
    pa, ra, ta, qa2, pb, rb, tb, qb2, rbuf, zbuf,
    lsem, qs, qr, lzs, lps, latr, pzs, pzr, pps, ppr, ws, wr, ats, atr,
    sa1, va1, sa2, va2, sb1, vb1, sb2, vb2, zs, zr, os_, or_,
):
    n_z = n_c // 2
    piece = rows // n_h
    n_lo = n_h // 2
    width = w2.shape[2]
    q_block = qbuf.shape[2]
    c = lax.axis_index("ctx")
    h = lax.axis_index("head")
    k = lax.rem(c, 2)
    z = lax.div(c, 2)
    partner = c + 1 - 2 * k
    z_of = [lax.rem(z + d, n_z) for d in range(n_z)]
    h_of = [lax.rem(h + e, n_h) for e in range(n_h)]
    hi, lo = lax.div(h, n_lo), lax.rem(h, n_lo)
    lo_of = [lax.rem(lo + e, n_lo) for e in range(n_lo)]
    c_of = [2 * zz + k for zz in z_of]

    def remote(src, dst, ssem, rsem, cc, hh):
        return pltpu.make_async_remote_copy(
            src_ref=src, dst_ref=dst, send_sem=ssem, recv_sem=rsem,
            device_id=(cc, hh), device_id_type=MESH,
        )

    def slot(cc):
        return latbuf.at[cc]

    barrier = pltpu.get_barrier_semaphore()
    for d in range(1, n_z):
        pl.semaphore_signal(barrier, inc=1, device_id=(c_of[d], h), device_id_type=MESH)
    for e in range(1, n_h):
        pl.semaphore_signal(barrier, inc=1, device_id=(c, h_of[e]), device_id_type=MESH)
    pl.semaphore_signal(barrier, inc=1, device_id=(partner, h), device_id_type=MESH)

    local = [
        pltpu.make_async_copy(qlat, qbuf.at[h], lsem.at[0]),
        pltpu.make_async_copy(wq, wq_v, lsem.at[1]),
        pltpu.make_async_copy(wkv, wkv_v, lsem.at[2]),
        pltpu.make_async_copy(lat, slot(c), lsem.at[3]),
        pltpu.make_async_copy(wout, w2.at[k], lsem.at[4]),
    ]
    for copy in local:
        copy.start()
    pl.semaphore_wait(barrier, n_z + n_h - 1)

    sends = []

    def send(*args):
        copy = remote(*args)
        copy.start()
        sends.append(copy)

    for e in range(1, n_h):
        send(qlat, qbuf.at[h], qs.at[e], qr.at[h], c, h_of[e])
    for d in range(n_z - 1, 0, -1):
        send(lat, slot(c), lzs.at[d], latr.at[c], c_of[d], h)
    send(lat, slot(c), lps.at[0], latr.at[c], partner, h)
    posbuf[k, z] = kpos[...]
    for d in range(1, n_z):
        send(kpos, posbuf.at[k, z], pzs.at[d], pzr.at[z], c_of[d], h)

    local[0].wait()
    local[1].wait()
    for e in range(1, n_h):
        remote(qlat, qbuf.at[h_of[e]], qs.at[e], qr.at[h_of[e]], c, h_of[e]).wait_recv()
    query = None
    for g in range(n_h):
        term = jnp.dot(qbuf[g], wq_v[g * q_block:(g + 1) * q_block, :], preferred_element_type=F32)
        query = term if query is None else query + term
    local[2].wait()
    for j in range(heads):
        base = j * (NOPE + ROPE)
        nope = query[:, base:base + NOPE].astype(BF16)
        main = dot_t(nope, wkv_v[:, j * 256:j * 256 + NOPE])
        lines = slice(j * rows, (j + 1) * rows)
        qa[lines, 0:KVL] = main.astype(BF16)
        rope = query[:, base + NOPE:base + NOPE + ROPE]
        half = ROPE // 2
        swapped = jnp.concatenate([rope[:, half:], rope[:, :half]], axis=1)
        rotated = rope * cos[...] + swapped * sin[...]
        qa[lines, KVL:LANES] = rotated.astype(BF16)

    for d in range(1, n_z):
        remote(lat, slot(c_of[d]), lzs.at[d], latr.at[c_of[d]], c_of[d], h).wait_recv()
        send(slot(c_of[d]), slot(c_of[d]), lps.at[d], latr.at[c_of[d]], partner, h)
    for d in range(1, n_z):
        remote(kpos, posbuf.at[k, z_of[d]], pzs.at[d], pzr.at[z_of[d]], c_of[d], h).wait_recv()
    send(posbuf.at[k], posbuf.at[k], pps, ppr, partner, h)
    send(wout, w2.at[k], ws, wr, partner, h)
    local[3].wait()
    for d in range(n_z):
        cc = 2 * z_of[d] + 1 - k
        remote(lat, slot(cc), lps.at[d], latr.at[cc], partner, h).wait_recv()

    remote(posbuf.at[1 - k], posbuf.at[1 - k], pps, ppr, partner, h).wait_recv()
    key_pos = jnp.concatenate([posbuf[cc % 2, cc // 2, 0:1, :] for cc in range(n_c)], axis=1)
    latents = jnp.concatenate([latbuf[cc] for cc in range(n_c)], axis=1)
    score[...] = jnp.dot(qa[...], latents, preferred_element_type=F32)
    visible = key_pos <= qpos[:, 0:1]
    sums = []
    for j in range(heads):
        lines = slice(j * rows, (j + 1) * rows)
        s = jnp.where(visible, score[lines, :] * softmax_scale, negative_fill)
        largest = jnp.max(s, axis=-1, keepdims=True)
        weights = jnp.where(visible, jnp.exp(s - largest), 0.0)
        sums.append(jnp.sum(weights, axis=-1, keepdims=True))
        prob[lines, :] = weights.astype(BF16)
    summed = dot_t(prob[...], latents[0:KVL, :])
    for j in range(heads):
        normed = (summed[j * rows:(j + 1) * rows, :] / sums[j]).astype(BF16)
        value = jnp.dot(normed, wkv_v[:, j * 256 + NOPE:(j + 1) * 256], preferred_element_type=F32)
        attbuf[z, :, j * VDIM:(j + 1) * VDIM] = value.astype(BF16)

    for d in range(n_z - 1, 0, -1):
        send(attbuf.at[z], attbuf.at[z], ats.at[d], atr.at[z], c_of[d], h)

    local[4].wait()
    remote(wout, w2.at[1 - k], ws, wr, partner, h).wait_recv()

    def project(d):
        zz = z_of[d]
        if d > 0:
            remote(attbuf.at[zz], attbuf.at[zz], ats.at[d], atr.at[zz], c_of[d], h).wait_recv()
        part = jnp.dot(attbuf[zz], w2[0], preferred_element_type=F32).astype(BF16)
        for i in range(n_h):
            pa[d, i % n_lo, i // n_lo] = part[i * piece:(i + 1) * piece, :]
        for e in range(1, n_lo):
            send(pa.at[d, lo_of[e]], ra.at[d, lo], sa1.at[d, e], va1.at[d, lo], c, hi * n_lo + lo_of[e])
        part = jnp.dot(attbuf[zz], w2[1], preferred_element_type=F32).astype(BF16)
        for i in range(n_h):
            pb[d, i // n_lo, i % n_lo] = part[i * piece:(i + 1) * piece, :]
        send(pb.at[d, 1 - hi], rb.at[d], sb1.at[d], vb1.at[d], c, (1 - hi) * n_lo + lo)

    def second(d):
        total = pa[d, lo].astype(F32)
        for e in range(1, n_lo):
            ll = lo_of[e]
            remote(pa.at[d, ll], ra.at[d, ll], sa1.at[d, e], va1.at[d, ll], c, hi * n_lo + ll).wait_recv()
            total = total + ra[d, ll].astype(F32)
        ta[d] = total.astype(BF16)
        send(ta.at[d, 1 - hi], qa2.at[d], sa2.at[d], va2.at[d], c, (1 - hi) * n_lo + lo)
        remote(pb.at[d, hi], rb.at[d], sb1.at[d], vb1.at[d], c, (1 - hi) * n_lo + lo).wait_recv()
        tb[d] = (pb[d, hi].astype(F32) + rb[d].astype(F32)).astype(BF16)
        for e in range(1, n_lo):
            send(tb.at[d, lo_of[e]], qb2.at[d, lo], sb2.at[d, e], vb2.at[d, lo], c, hi * n_lo + lo_of[e])

    def third(d):
        remote(ta.at[d, hi], qa2.at[d], sa2.at[d], va2.at[d], c, (1 - hi) * n_lo + lo).wait_recv()
        first = (ta[d, hi].astype(F32) + qa2[d].astype(F32)).astype(BF16)
        total = tb[d, lo].astype(F32)
        for e in range(1, n_lo):
            ll = lo_of[e]
            remote(tb.at[d, ll], qb2.at[d, ll], sb2.at[d, e], vb2.at[d, ll], c, hi * n_lo + ll).wait_recv()
            total = total + qb2[d, ll].astype(F32)
        if d == 0:
            zbuf[z, :, 0:width] = first
            zbuf[z, :, width:] = total.astype(BF16)
        else:
            rbuf[d, :, 0:width] = first
            rbuf[d, :, width:] = total.astype(BF16)
            send(rbuf.at[d], zbuf.at[z], zs.at[d], zr.at[z], c_of[d], h)

    def deliver(d):
        zz = z_of[(n_z - d) % n_z]
        if d > 0:
            remote(rbuf.at[0], zbuf.at[zz], zs.at[0], zr.at[zz], partner, h).wait_recv()

        @pl.when(zz != h)
        def _():
            remote(zbuf.at[zz], out.at[h], os_.at[d], or_.at[h], c, zz).start()

        @pl.when(zz == h)
        def _():
            out[h] = zbuf[zz]

    def delivered(d):
        zz = z_of[(n_z - d) % n_z]

        @pl.when(zz != h)
        def _():
            remote(zbuf.at[zz], out.at[h], os_.at[d], or_.at[h], c, zz).wait_send()

    for d in range(n_z + 3):
        if d < n_z:
            project(d)
        if 1 <= d <= n_z:
            second(d - 1)
        if 2 <= d <= n_z + 1:
            third(d - 2)
        if d >= 3:
            deliver(d - 3)
    for e in range(1, n_h):
        hh = h_of[e]
        remote(zbuf.at[0], out.at[hh], os_.at[0], or_.at[hh], c, hh).wait_recv()
    for d in range(n_z):
        delivered(d)
    for copy in sends:
        copy.wait_send()


def shards(n_c, n_h, q_latent, latent_cache, w_q_up, w_kv_up, w_out, token_pos, start_offset):
    rows, q_block = q_latent.shape
    heads = w_q_up.shape[1] // (NOPE + ROPE)
    n_z, n_lo = n_c // 2, n_h // 2
    assert n_z == n_h
    keys = n_c * rows
    width = w_out.shape[1]
    piece = rows // n_h
    absolute = (token_pos + start_offset[0]).astype(F32)
    freqs = rope_base ** (-jnp.arange(ROPE // 2, dtype=F32) * 2.0 / ROPE)
    angle = absolute[:, None] * freqs[None, :]
    cosine, sine = jnp.cos(angle), jnp.sin(angle)
    cos = jnp.concatenate([cosine, cosine], axis=1)
    sin = jnp.concatenate([-sine, sine], axis=1)
    qpos = jnp.broadcast_to(token_pos.astype(F32)[:, None], (rows, 128))
    kpos = jnp.broadcast_to(token_pos.astype(F32)[None, :], (8, rows))
    dma = pltpu.SemaphoreType.DMA
    anywhere = pl.BlockSpec(memory_space=pltpu.HBM)
    vmem = pl.BlockSpec(memory_space=pltpu.VMEM)
    result = pl.pallas_call(
        functools.partial(kernel, n_c, n_h, heads, rows),
        out_shape=jax.ShapeDtypeStruct((n_h, piece, 2 * width), BF16),
        in_specs=[anywhere] * 5 + [vmem] * 4,
        out_specs=vmem,
        scratch_shapes=[
            pltpu.VMEM(w_q_up.shape, BF16),
            pltpu.VMEM(w_kv_up.shape, BF16),
            pltpu.VMEM((2,) + w_out.shape, BF16),
            pltpu.VMEM((n_h, rows, q_block), BF16),
            pltpu.VMEM((n_c, LANES, rows), BF16),
            pltpu.VMEM((2, n_z, 8, rows), F32),
            pltpu.VMEM((heads * rows, LANES), BF16),
            pltpu.VMEM((heads * rows, keys), F32),
            pltpu.VMEM((heads * rows, keys), BF16),
            pltpu.VMEM((n_z, rows, heads * VDIM), BF16),
            pltpu.VMEM((n_z, n_lo, 2, piece, width), BF16),
            pltpu.VMEM((n_z, n_lo, 2, piece, width), BF16),
            pltpu.VMEM((n_z, 2, piece, width), BF16),
            pltpu.VMEM((n_z, piece, width), BF16),
            pltpu.VMEM((n_z, 2, n_lo, piece, width), BF16),
            pltpu.VMEM((n_z, n_lo, piece, width), BF16),
            pltpu.VMEM((n_z, n_lo, piece, width), BF16),
            pltpu.VMEM((n_z, n_lo, piece, width), BF16),
            pltpu.VMEM((n_z, piece, 2 * width), BF16),
            pltpu.VMEM((n_z, piece, 2 * width), BF16),
            dma((5,)),
            dma((n_h,)), dma((n_h,)),
            dma((n_z,)), dma((n_z,)), dma((n_c,)),
            dma((n_z,)), dma((n_z,)), dma, dma,
            dma, dma,
            dma((n_z,)), dma((n_z,)),
            dma((n_z, n_lo)), dma((n_z, n_lo)), dma((n_z,)), dma((n_z,)),
            dma((n_z,)), dma((n_z,)), dma((n_z, n_lo)), dma((n_z, n_lo)),
            dma((n_z,)), dma((n_z,)),
            dma((n_z,)), dma((n_h,)),
        ],
        compiler_params=pltpu.CompilerParams(
            collective_id=0, has_side_effects=True, vmem_limit_bytes=67043328 - (768 << 10)
        ),
        name="mla",
    )(q_latent, latent_cache.T, w_q_up, w_kv_up, w_out, cos, sin, kpos, qpos)
    return result.reshape(rows, 2 * width)


def solution(mesh):
    in_specs = (
        P("ctx", "head"),
        P("ctx", None),
        P(None, "head"),
        P(None, "head"),
        P("head", "ctx"),
        P("ctx"),
        P(),
    )
    out_specs = P("ctx", "head")
    body = functools.partial(shards, mesh.shape["ctx"], mesh.shape["head"])
    return jax.shard_map(body, mesh=mesh, in_specs=in_specs, out_specs=out_specs, check_vma=False)
```

```python
import functools

import jax
import jax.numpy as jnp
from jax import lax
from jax.experimental import pallas as pl
from jax.experimental.pallas import tpu as pltpu
from jax.sharding import PartitionSpec as P

KVL = 512
NOPE = 128
ROPE = 64
VDIM = 128
LANES = KVL + ROPE

negative_fill = -1e30
softmax_scale = 0.135
rope_base = 10000.0
F32 = jnp.float32
BF16 = jnp.bfloat16
MESH = pl.DeviceIdType.MESH


def dot_t(a, b):
    return lax.dot_general(a, b, (((1,), (1,)), ((), ())), preferred_element_type=F32)


def kernel(
    n_c, n_h, heads, rows,
    qlat, lat, wq, wkv, wout, cos, sin, kpos,
    out,
    wq_v, wkv_v, w2, qbuf, latbuf, posbuf, qa, score, prob, attbuf,
    pa, ra, ta, qa2, pb, rb, tb, qb2, rbuf, zbuf,
    lsem, qs, qr, lzs, lps, latr, xzs, xzr, xps, xpr, pzs, pzr, pps, ppr, ws, wr, ats, atr,
    sa1, va1, sa2, va2, sb1, vb1, sb2, vb2, zs, zr, os_, or_,
):
    n_z = n_c // 2
    piece = rows // n_h
    n_lo = n_h // 2
    width = w2.shape[2]
    q_block = qbuf.shape[2]
    c = lax.axis_index("ctx")
    h = lax.axis_index("head")
    k = lax.rem(c, 2)
    z = lax.div(c, 2)
    partner = c + 1 - 2 * k
    z_of = [lax.rem(z + d, n_z) for d in range(n_z)]
    h_of = [lax.rem(h + e, n_h) for e in range(n_h)]
    hi, lo = lax.div(h, n_lo), lax.rem(h, n_lo)
    lo_of = [lax.rem(lo + e, n_lo) for e in range(n_lo)]
    c_of = [2 * zz + k for zz in z_of]

    def remote(src, dst, ssem, rsem, cc, hh):
        return pltpu.make_async_remote_copy(
            src_ref=src, dst_ref=dst, send_sem=ssem, recv_sem=rsem,
            device_id=(cc, hh), device_id_type=MESH,
        )

    def slot(cc):
        return latbuf.at[cc]

    barrier = pltpu.get_barrier_semaphore()
    for d in range(1, n_z):
        pl.semaphore_signal(barrier, inc=1, device_id=(c_of[d], h), device_id_type=MESH)
    for e in range(1, n_h):
        pl.semaphore_signal(barrier, inc=1, device_id=(c, h_of[e]), device_id_type=MESH)
    pl.semaphore_signal(barrier, inc=1, device_id=(partner, h), device_id_type=MESH)

    local = [
        pltpu.make_async_copy(qlat, qbuf.at[h], lsem.at[0]),
        pltpu.make_async_copy(wq, wq_v, lsem.at[1]),
        pltpu.make_async_copy(wkv, wkv_v, lsem.at[2]),
        pltpu.make_async_copy(lat, slot(c), lsem.at[3]),
        pltpu.make_async_copy(wout, w2.at[k], lsem.at[4]),
    ]
    for copy in local:
        copy.start()
    pl.semaphore_wait(barrier, n_z + n_h - 1)

    third_rows = LANES // 3
    odd = lax.rem(lo, 2)
    pair = hi * n_lo + lo + 1 - 2 * odd
    mine = pl.ds(pl.multiple_of(odd * third_rows, third_rows), third_rows)
    other = pl.ds(pl.multiple_of((1 - odd) * third_rows, third_rows), third_rows)
    both = pl.ds(2 * third_rows, third_rows)
    sends = []

    def send(*args):
        copy = remote(*args)
        copy.start()
        sends.append(copy)

    for e in range(1, n_h):
        send(qlat, qbuf.at[h], qs.at[e], qr.at[h], c, h_of[e])
    for d in range(n_z - 1, 0, -1):
        send(lat.at[mine, :], latbuf.at[c, mine, :], xzs.at[d], xzr.at[z], c_of[d], h)
    for d in range(n_z - 1, 0, -1):
        send(lat.at[both, :], latbuf.at[c, both, :], lzs.at[d], latr.at[c], c_of[d], h)
    send(lat, slot(c), lps.at[0], latr.at[c], partner, h)
    posbuf[k, z] = kpos[...]
    for d in range(1, n_z):
        send(kpos, posbuf.at[k, z], pzs.at[d], pzr.at[z], c_of[d], h)

    for d in range(1, n_z):
        cc = c_of[d]
        remote(lat.at[mine, :], latbuf.at[cc, mine, :], xzs.at[d], xzr.at[z_of[d]], cc, h).wait_recv()
        send(latbuf.at[cc, mine, :], latbuf.at[cc, mine, :], xps.at[d], xpr.at[z_of[d]], c, pair)

    local[0].wait()
    local[1].wait()
    for e in range(1, n_h):
        remote(qlat, qbuf.at[h_of[e]], qs.at[e], qr.at[h_of[e]], c, h_of[e]).wait_recv()
    query = None
    for g in range(n_h):
        term = jnp.dot(qbuf[g], wq_v[g * q_block:(g + 1) * q_block, :], preferred_element_type=F32)
        query = term if query is None else query + term
    local[2].wait()
    for j in range(heads):
        base = j * (NOPE + ROPE)
        nope = query[:, base:base + NOPE].astype(BF16)
        main = dot_t(nope, wkv_v[:, j * 256:j * 256 + NOPE])
        lines = slice(j * rows, (j + 1) * rows)
        qa[lines, 0:KVL] = main.astype(BF16)
        rope = query[:, base + NOPE:base + NOPE + ROPE]
        half = ROPE // 2
        swapped = jnp.concatenate([rope[:, half:], rope[:, :half]], axis=1)
        rotated = rope * cos[...] + swapped * sin[...]
        qa[lines, KVL:LANES] = rotated.astype(BF16)

    for d in range(1, n_z):
        cc = c_of[d]
        remote(lat.at[both, :], latbuf.at[cc, both, :], lzs.at[d], latr.at[cc], cc, h).wait_recv()
        remote(
            latbuf.at[cc, other, :], latbuf.at[cc, other, :], xps.at[d], xpr.at[z_of[d]], c, pair
        ).wait_recv()
        send(slot(c_of[d]), slot(c_of[d]), lps.at[d], latr.at[c_of[d]], partner, h)
    for d in range(1, n_z):
        remote(kpos, posbuf.at[k, z_of[d]], pzs.at[d], pzr.at[z_of[d]], c_of[d], h).wait_recv()
    send(posbuf.at[k], posbuf.at[k], pps, ppr, partner, h)
    send(wout, w2.at[k], ws, wr, partner, h)
    local[3].wait()
    for d in range(n_z):
        cc = 2 * z_of[d] + 1 - k
        remote(lat, slot(cc), lps.at[d], latr.at[cc], partner, h).wait_recv()

    remote(posbuf.at[1 - k], posbuf.at[1 - k], pps, ppr, partner, h).wait_recv()
    key_pos = jnp.concatenate([posbuf[cc % 2, cc // 2, 0:1, :] for cc in range(n_c)], axis=1)
    latents = jnp.concatenate([latbuf[cc] for cc in range(n_c)], axis=1)
    score[...] = jnp.dot(qa[...], latents, preferred_element_type=F32)
    visible = key_pos <= jnp.transpose(kpos[...])[:, 0:1]
    sums = []
    for j in range(heads):
        lines = slice(j * rows, (j + 1) * rows)
        s = jnp.where(visible, score[lines, :] * softmax_scale, negative_fill)
        largest = jnp.max(s, axis=-1, keepdims=True)
        weights = jnp.where(visible, jnp.exp(s - largest), 0.0)
        sums.append(jnp.sum(weights, axis=-1, keepdims=True))
        prob[lines, :] = weights.astype(BF16)
    summed = dot_t(prob[...], latents[0:KVL, :])
    for j in range(heads):
        normed = (summed[j * rows:(j + 1) * rows, :] / sums[j]).astype(BF16)
        value = jnp.dot(normed, wkv_v[:, j * 256 + NOPE:(j + 1) * 256], preferred_element_type=F32)
        attbuf[z, :, j * VDIM:(j + 1) * VDIM] = value.astype(BF16)

    for d in range(n_z - 1, 0, -1):
        send(attbuf.at[z], attbuf.at[z], ats.at[d], atr.at[z], c_of[d], h)

    local[4].wait()
    remote(wout, w2.at[1 - k], ws, wr, partner, h).wait_recv()

    def project(d):
        zz = z_of[d]
        if d > 0:
            remote(attbuf.at[zz], attbuf.at[zz], ats.at[d], atr.at[zz], c_of[d], h).wait_recv()
        part = jnp.dot(attbuf[zz], w2[0], preferred_element_type=F32).astype(BF16)
        for i in range(n_h):
            pa[d, i % n_lo, i // n_lo] = part[i * piece:(i + 1) * piece, :]
        for e in range(1, n_lo):
            send(pa.at[d, lo_of[e]], ra.at[d, lo], sa1.at[d, e], va1.at[d, lo], c, hi * n_lo + lo_of[e])
        part = jnp.dot(attbuf[zz], w2[1], preferred_element_type=F32).astype(BF16)
        for i in range(n_h):
            pb[d, i // n_lo, i % n_lo] = part[i * piece:(i + 1) * piece, :]
        send(pb.at[d, 1 - hi], rb.at[d], sb1.at[d], vb1.at[d], c, (1 - hi) * n_lo + lo)

    def second(d):
        total = pa[d, lo].astype(F32)
        for e in range(1, n_lo):
            ll = lo_of[e]
            remote(pa.at[d, ll], ra.at[d, ll], sa1.at[d, e], va1.at[d, ll], c, hi * n_lo + ll).wait_recv()
            total = total + ra[d, ll].astype(F32)
        ta[d] = total.astype(BF16)
        send(ta.at[d, 1 - hi], qa2.at[d], sa2.at[d], va2.at[d], c, (1 - hi) * n_lo + lo)
        remote(pb.at[d, hi], rb.at[d], sb1.at[d], vb1.at[d], c, (1 - hi) * n_lo + lo).wait_recv()
        tb[d] = (pb[d, hi].astype(F32) + rb[d].astype(F32)).astype(BF16)
        for e in range(1, n_lo):
            send(tb.at[d, lo_of[e]], qb2.at[d, lo], sb2.at[d, e], vb2.at[d, lo], c, hi * n_lo + lo_of[e])

    def third(d):
        remote(ta.at[d, hi], qa2.at[d], sa2.at[d], va2.at[d], c, (1 - hi) * n_lo + lo).wait_recv()
        first = (ta[d, hi].astype(F32) + qa2[d].astype(F32)).astype(BF16)
        total = tb[d, lo].astype(F32)
        for e in range(1, n_lo):
            ll = lo_of[e]
            remote(tb.at[d, ll], qb2.at[d, ll], sb2.at[d, e], vb2.at[d, ll], c, hi * n_lo + ll).wait_recv()
            total = total + qb2[d, ll].astype(F32)
        if d == 0:
            zbuf[z, :, 0:width] = first
            zbuf[z, :, width:] = total.astype(BF16)
        else:
            rbuf[d, :, 0:width] = first
            rbuf[d, :, width:] = total.astype(BF16)
            send(rbuf.at[d], zbuf.at[z], zs.at[d], zr.at[z], c_of[d], h)

    def deliver(d):
        zz = z_of[(n_z - d) % n_z]
        if d > 0:
            remote(rbuf.at[0], zbuf.at[zz], zs.at[0], zr.at[zz], partner, h).wait_recv()

        @pl.when(zz != h)
        def _():
            remote(zbuf.at[zz], out.at[h], os_.at[d], or_.at[h], c, zz).start()

        @pl.when(zz == h)
        def _():
            out[h] = zbuf[zz]

    def delivered(d):
        zz = z_of[(n_z - d) % n_z]

        @pl.when(zz != h)
        def _():
            remote(zbuf.at[zz], out.at[h], os_.at[d], or_.at[h], c, zz).wait_send()

    for d in range(n_z + 3):
        if d < n_z:
            project(d)
        if 1 <= d <= n_z:
            second(d - 1)
        if 2 <= d <= n_z + 1:
            third(d - 2)
        if d >= 3:
            deliver(d - 3)
    for e in range(1, n_h):
        hh = h_of[e]
        remote(zbuf.at[0], out.at[hh], os_.at[0], or_.at[hh], c, hh).wait_recv()
    for d in range(n_z):
        delivered(d)
    for copy in sends:
        copy.wait_send()


def shards(n_c, n_h, q_latent, latent_cache, w_q_up, w_kv_up, w_out, token_pos, start_offset):
    rows, q_block = q_latent.shape
    heads = w_q_up.shape[1] // (NOPE + ROPE)
    n_z, n_lo = n_c // 2, n_h // 2
    assert n_z == n_h
    keys = n_c * rows
    width = w_out.shape[1]
    piece = rows // n_h
    absolute = (token_pos + start_offset[0]).astype(F32)
    freqs = rope_base ** (-jnp.arange(ROPE // 2, dtype=F32) * 2.0 / ROPE)
    angle = absolute[:, None] * freqs[None, :]
    cosine, sine = jnp.cos(angle), jnp.sin(angle)
    cos = jnp.concatenate([cosine, cosine], axis=1)
    sin = jnp.concatenate([-sine, sine], axis=1)
    kpos = jnp.broadcast_to(token_pos.astype(F32)[None, :], (8, rows))
    dma = pltpu.SemaphoreType.DMA
    anywhere = pl.BlockSpec(memory_space=pltpu.HBM)
    vmem = pl.BlockSpec(memory_space=pltpu.VMEM)
    result = pl.pallas_call(
        functools.partial(kernel, n_c, n_h, heads, rows),
        out_shape=jax.ShapeDtypeStruct((n_h, piece, 2 * width), BF16),
        in_specs=[anywhere] * 5 + [vmem] * 3,
        out_specs=vmem,
        scratch_shapes=[
            pltpu.VMEM(w_q_up.shape, BF16),
            pltpu.VMEM(w_kv_up.shape, BF16),
            pltpu.VMEM((2,) + w_out.shape, BF16),
            pltpu.VMEM((n_h, rows, q_block), BF16),
            pltpu.VMEM((n_c, LANES, rows), BF16),
            pltpu.VMEM((2, n_z, 8, rows), F32),
            pltpu.VMEM((heads * rows, LANES), BF16),
            pltpu.VMEM((heads * rows, keys), F32),
            pltpu.VMEM((heads * rows, keys), BF16),
            pltpu.VMEM((n_z, rows, heads * VDIM), BF16),
            pltpu.VMEM((n_z, n_lo, 2, piece, width), BF16),
            pltpu.VMEM((n_z, n_lo, 2, piece, width), BF16),
            pltpu.VMEM((n_z, 2, piece, width), BF16),
            pltpu.VMEM((n_z, piece, width), BF16),
            pltpu.VMEM((n_z, 2, n_lo, piece, width), BF16),
            pltpu.VMEM((n_z, n_lo, piece, width), BF16),
            pltpu.VMEM((n_z, n_lo, piece, width), BF16),
            pltpu.VMEM((n_z, n_lo, piece, width), BF16),
            pltpu.VMEM((n_z, piece, 2 * width), BF16),
            pltpu.VMEM((n_z, piece, 2 * width), BF16),
            dma((5,)),
            dma((n_h,)), dma((n_h,)),
            dma((n_z,)), dma((n_z,)), dma((n_c,)),
            dma((n_z,)), dma((n_z,)), dma((n_z,)), dma((n_z,)),
            dma((n_z,)), dma((n_z,)), dma, dma,
            dma, dma,
            dma((n_z,)), dma((n_z,)),
            dma((n_z, n_lo)), dma((n_z, n_lo)), dma((n_z,)), dma((n_z,)),
            dma((n_z,)), dma((n_z,)), dma((n_z, n_lo)), dma((n_z, n_lo)),
            dma((n_z,)), dma((n_z,)),
            dma((n_z,)), dma((n_h,)),
        ],
        compiler_params=pltpu.CompilerParams(
            collective_id=0, has_side_effects=True, vmem_limit_bytes=67043328 - (768 << 10)
        ),
        name="mla",
    )(q_latent, latent_cache.T, w_q_up, w_kv_up, w_out, cos, sin, kpos)
    return result.reshape(rows, 2 * width)


def solution(mesh):
    in_specs = (
        P("ctx", "head"),
        P("ctx", None),
        P(None, "head"),
        P(None, "head"),
        P("head", "ctx"),
        P("ctx"),
        P(),
    )
    out_specs = P("ctx", "head")
    body = functools.partial(shards, mesh.shape["ctx"], mesh.shape["head"])
    return jax.shard_map(body, mesh=mesh, in_specs=in_specs, out_specs=out_specs, check_vma=False)
```
